256 devices in a mesh: dp: 8 (over x, core), ctx: 32 (over y, z).
Axes of the slice: x: 4, y: 4, z: 8, core: 2. Of those that a mesh axis runs over, the one named last changes fastest.
Arguments:
- merged_grad: bfloat16 [32768, 1792], P(('dp', 'ctx')), may hold values from -6 to 6
- merged_owner: int32 [32768, 1], P(('dp', 'ctx')), may hold values from 0 to 31; in each aligned block of 128 rows (0 to 127, 128 to 255, ...) at most 8 rows name the same one
- merger_pre: bfloat16 [65536, 2560], P(('dp', 'ctx')), may hold values from -24 to 24
- fc2_weight: bfloat16 [2560, 1792], P('ctx'), may hold values from -0.125 to 0.125
- query: bfloat16 [65536, 1280], P(('dp', 'ctx')), may hold values from -32 to 32
- key_states: bfloat16 [65536, 1280], P(('dp', 'ctx')), may hold values from -32 to 32
- value_states: bfloat16 [65536, 1280], P(('dp', 'ctx')), may hold values from -6 to 6
- out_grad: bfloat16 [65536, 1280], P(('dp', 'ctx')), may hold values from -6 to 6
- position: int32 [2, 65536], P(None, ('dp', 'ctx')), may hold values from 0 to 63, as said below
Outputs:
- hidden_grad: bfloat16 [65536, 2560], P(('dp', 'ctx'))
- weight_grad: float32 [2560, 1792], P('ctx', 'dp')
- query_grad: bfloat16 [65536, 1280], P(('dp', 'ctx'))
- key_grad: bfloat16 [65536, 1280], P(('dp', 'ctx'))
- value_grad: bfloat16 [65536, 1280], P(('dp', 'ctx'))
The draws below stay inside these ranges and needn't reach their ends.
Inputs may be any that keep to these rules, and one draw needn't show every extreme that they name: `merged_owner`: in each device's block of 128 rows no owner is named more than 8 times. `position`: each window of 64 consecutive patches covers an aligned square of 8 by 8 grid positions, row by row.
All inputs are finite; a program needn't handle non-finite values.
Results may differ from the reference program's by a relative error of at most 0.0017.
The reference program's roundings to bfloat16 on the way (of `slotted`, `act`, `q_rot`, `k_rot`, `probs_b` and `score_grad`) count: a program that leaves them out, or rounds other values in their place, can miss the bound.
Values may be sent and summed in bfloat16 or wider, within the bound.
No kernel may reach another device: no remote copies, remote signals or barrier semaphores. Data moves between devices by JAX's collectives and lax.ppermute only.
A program may use at most 128 MiB of HBM per device.

```python
import math
import jax
import jax.numpy as jnp
import numpy as np
from jax import lax

D = 1280
HEADS = 16
HEAD = 80
WIN_SIDE = 8
WIN = 64
HID = 2560
OUTW = 1792
G_DEV = 128
PATCH_DEV = 256
CAP = 8
SLOTS = 256
TOKENS = 32768
ALLSLOTS = 65536
PATCHES = 65536
N_DP = 8
N_CTX = 32


def window_positions(key):
    pkey = jax.random.fold_in(key, 7)
    windows = PATCHES // WIN
    corner = jax.random.randint(pkey, (2, windows), 0, WIN_SIDE, dtype=jnp.int32)
    inside = jnp.arange(WIN, dtype=jnp.int32)
    rows = corner[0][:, None] * WIN_SIDE + inside[None, :] // WIN_SIDE
    cols = corner[1][:, None] * WIN_SIDE + inside[None, :] % WIN_SIDE
    return jnp.stack([rows.reshape(-1), cols.reshape(-1)])


def drawn_pair(key):
    query = jax.random.normal(jax.random.fold_in(key, 11), (PATCHES, HEADS, HEAD), jnp.float32)
    keys = jax.random.normal(jax.random.fold_in(key, 12), (PATCHES, HEADS, HEAD), jnp.float32)
    return (query.reshape(PATCHES, D), keys.reshape(PATCHES, D))


def draw_query(key, part):
    return drawn_pair(key)[0].astype(jnp.bfloat16)


def draw_key_states(key, part):
    return drawn_pair(key)[1].astype(jnp.bfloat16)


def draw_position(key, part):
    return window_positions(key)


def with_spikes(entries, rng, source, target, parts, factor):
    def block_of(dim):
        return (jnp.arange(entries.shape[dim]) // (entries.shape[dim] // parts)).reshape((-1,) + (1,) * (entries.ndim - 1 - dim))

    first = jax.random.permutation(rng, parts)[block_of(target)]
    far = (block_of(target) + parts // 2) % parts
    return jnp.where((block_of(source) == first) | (block_of(source) == far), factor * entries, entries)


def block_scale(key, dims, split, low, top_value):
    gain, own = 1.0, jax.random.fold_in(key, 6)
    for dim, blocks in split:
        steps = jnp.exp(jax.random.uniform(jax.random.fold_in(own, dim), (blocks,), jnp.float32, low / len(split), top_value / len(split)))
        gain = gain * jnp.repeat(steps, dims[dim] // blocks).reshape([-1 if axis == dim else 1 for axis in range(len(dims))])
    return gain


def routed_block(key, own, number, rows, amount, top, reach, lean):
    sequence = jax.random.permutation(key, amount)
    heavy_load, usual = load_shares(amount, rows * top, reach, lean, True), load_shares(amount, rows * top, reach, lean, False)
    places = jnp.arange(amount)

    def named(tallies, turn):
        used = int((tallies > 0).sum())
        fixed = max(1, used // 4)
        moved = fixed + (places - fixed + turn * (used - fixed)) % max(1, amount - fixed)
        return jnp.zeros((amount,), jnp.int32).at[sequence[jnp.where(places < fixed, places, moved)]].set(jnp.asarray(tallies, jnp.int32))

    tallies = jnp.where(number % 4 == 0, named(heavy_load, number // 4), named(usual, number - number // 4 - 1))
    mixed = jax.random.permutation(jax.random.fold_in(own, 3), amount)
    source_of, sink = mixed[0:amount // 2 * 2:2], mixed[1:amount // 2 * 2:2]
    slack = jnp.minimum(tallies[source_of] - 1, reach - tallies[sink]) // 2
    slack = jnp.where((source_of == sequence[0]) | (sink == sequence[0]) | (tallies[sink] == 0), 0, jnp.maximum(slack, 0))
    moved = jax.random.randint(jax.random.fold_in(own, 4), (amount // 2,), 0, 1 << 20) % (slack + 1)
    tallies = tallies.at[source_of].add(-moved).at[sink].add(moved)
    members = jnp.searchsorted(jnp.cumsum(tallies), jnp.arange(rows * top), side="right").astype(jnp.int32)
    grid = members.reshape(top, rows).T
    grid = grid[jax.random.permutation(jax.random.fold_in(own, 1), rows)]
    turn = jax.random.randint(jax.random.fold_in(own, 2), (rows, 1), 0, top)
    return jnp.take_along_axis(grid, (jnp.arange(top)[None, :] + turn) % top, axis=1)


def load_shares(count, total, bound, skew, full):
    weights = [(1 << 20) // math.isqrt(standing ** skew) + 1 for standing in range(1, count + 1)]
    largest = bound if full else min(bound, max(-(-total // count), total * weights[0] // sum(weights)))
    least = 1 if total - largest >= count - 1 else 0
    given, spare = [largest] + [least] * (count - 1), total - largest - least * (count - 1)
    while spare > 0:
        movable = [i for i in range(1, count) if given[i] < largest] or [i for i in range(1, count) if given[i] < bound]
        pool, left = sum([weights[i] for i in movable]), spare
        for i in movable:
            extra = min(bound - given[i], max(1, left * weights[i] // pool), spare)
            given[i] = given[i] + extra
            spare = spare - extra
    return np.array(given)


def noise(stream_key, dims, deviation, limit, cuts=(), held_as=jnp.bfloat16):
    values = deviation * jax.random.normal(stream_key, dims, jnp.float32)
    if cuts:
        values = values * block_scale(stream_key, dims, cuts, -0.22, 0.18)
    return jnp.clip(values, -limit, limit).astype(held_as)


def gaussian_with(key, extent, width, most, shards, heavy, kind=jnp.bfloat16):
    values = width * jax.random.normal(key, extent, jnp.float32)
    if shards:
        values = values * block_scale(key, extent, shards, -0.22, 0.18)
    return jnp.clip(with_spikes(values, jax.random.fold_in(key, 3), *heavy), -most, most).astype(kind)


def setup_inputs(seed: int = 0) -> dict:
    splits = jax.random.split(jax.random.key(seed), 10)
    merged_grad = noise(splits[0], (TOKENS, OUTW), 1.0, 6.0, ((0, 256),))
    merged_owner_keys = jax.random.split(jax.random.fold_in(splits[1], 1), TOKENS // G_DEV)
    merged_owner_turns = jax.random.permutation(jax.random.fold_in(splits[1], 3), TOKENS // G_DEV)
    merged_owner = jax.vmap(lambda own, number: routed_block(jax.random.fold_in(splits[1], 2), own, number, G_DEV, N_CTX, 1, CAP, 2))(merged_owner_keys, merged_owner_turns).reshape((TOKENS, 1))
    merger_pre = gaussian_with(splits[2], (ALLSLOTS, HID), 1.0, 24.0, ((0, 256),), (0, 1, 256, 6.0))
    fc2_weight = noise(splits[3], (HID, OUTW), HID ** -0.5, 0.125, ((0, 32),))
    query = draw_query(jax.random.fold_in(splits[9], 71), 0)
    key_states = draw_key_states(jax.random.fold_in(splits[9], 71), 0)
    value_states = noise(splits[6], (PATCHES, D), 1.0, 6.0, ((0, 256),))
    out_grad = noise(splits[7], (PATCHES, D), 1.0, 6.0, ((0, 256),))
    position = draw_position(jax.random.fold_in(splits[9], 71), 0)
    return {"merged_grad": merged_grad, "merged_owner": merged_owner, "merger_pre": merger_pre, "fc2_weight": fc2_weight, "query": query, "key_states": key_states, "value_states": value_states, "out_grad": out_grad, "position": position}


def rope_angles(position, head_size):
    quarter = head_size // 4
    freq = 1.0 / (10000.0 ** (jnp.arange(quarter, dtype=jnp.float32) * (4.0 / head_size)))
    rows = position[0].astype(jnp.float32)[:, None] * freq[None, :]
    cols = position[1].astype(jnp.float32)[:, None] * freq[None, :]
    return jnp.concatenate([rows, cols], axis=1)


def rotate(values, angles, sign):
    half = values.shape[-1] // 2
    cosine = jnp.cos(angles)[:, None, :]
    sine = sign * jnp.sin(angles)[:, None, :]
    first = values[..., :half]
    second = values[..., half:]
    return jnp.concatenate([first * cosine - second * sine, second * cosine + first * sine], axis=-1)


def attention_block(query, key_states, value_states, out_grad, position):
    count = query.shape[0]
    windows = count // WIN
    angles = rope_angles(position, HEAD)
    shaped = (count, HEADS, HEAD)
    grouped = (windows, WIN, HEADS, HEAD)
    q_rot = rotate(query.astype(jnp.float32).reshape(shaped), angles, 1.0).astype(jnp.bfloat16)
    k_rot = rotate(key_states.astype(jnp.float32).reshape(shaped), angles, 1.0).astype(jnp.bfloat16)
    q_full = lax.optimization_barrier(q_rot).reshape(grouped).astype(jnp.float32)
    k_full = lax.optimization_barrier(k_rot).reshape(grouped).astype(jnp.float32)
    v_full = value_states.reshape(grouped).astype(jnp.float32)
    g_full = out_grad.reshape(grouped).astype(jnp.float32)
    factor = HEAD ** -0.5
    scores = jnp.einsum("wqhd,wkhd->whqk", q_full, k_full) * factor
    probs = jax.nn.softmax(scores, axis=-1)
    probs_b = lax.optimization_barrier(probs.astype(jnp.bfloat16)).astype(jnp.float32)
    output = jnp.einsum("whqk,wkhd->wqhd", probs_b, v_full)
    value_grad = jnp.einsum("whqk,wqhd->wkhd", probs_b, g_full).astype(jnp.bfloat16)
    prob_grad = jnp.einsum("wqhd,wkhd->whqk", g_full, v_full)
    delta = jnp.transpose(jnp.sum(g_full * output, axis=-1), (0, 2, 1))[..., None]
    score_grad = (probs * (prob_grad - delta)).astype(jnp.bfloat16)
    score_full = lax.optimization_barrier(score_grad).astype(jnp.float32)
    q_grad = jnp.einsum("whqk,wkhd->wqhd", score_full, k_full) * factor
    k_grad = jnp.einsum("whqk,wqhd->wkhd", score_full, q_full) * factor
    query_grad = rotate(q_grad.reshape(shaped), angles, -1.0).astype(jnp.bfloat16).reshape(count, D)
    key_grad = rotate(k_grad.reshape(shaped), angles, -1.0).astype(jnp.bfloat16).reshape(count, D)
    return query_grad, key_grad, value_grad.reshape(count, D)


def reference(merged_grad, merged_owner, merger_pre, fc2_weight, query, key_states, value_states, out_grad, position):
    group_rows = N_CTX * G_DEV
    owner = merged_owner[:, 0].reshape(N_DP, group_rows)
    owners = jnp.arange(N_CTX, dtype=jnp.int32)
    onehot = (owner[:, :, None] == owners[None, None, :]).astype(jnp.int32)
    running = jnp.cumsum(onehot, axis=1, dtype=jnp.int32)
    slot = jnp.sum(running * onehot, axis=2, dtype=jnp.int32) - 1
    group = jnp.arange(N_DP, dtype=jnp.int32)[:, None]
    target = ((group * N_CTX + owner) * SLOTS + slot).reshape(-1).astype(jnp.int32)
    slotted = jnp.zeros((N_DP * N_CTX * SLOTS, OUTW), jnp.bfloat16).at[target].set(merged_grad)

    def merger_group(carry, items):
        slotted_part, pre_part = items
        pre = pre_part.astype(jnp.float32)
        cdf = 0.5 * (1.0 + lax.erf(pre * (0.5 ** 0.5)))
        act = (pre * cdf).astype(jnp.bfloat16)
        slope = cdf + pre * jnp.exp(-0.5 * pre * pre) * ((2.0 * math.pi) ** -0.5)
        linear = jnp.dot(slotted_part, fc2_weight.T, preferred_element_type=jnp.float32)
        hidden = (linear * slope).astype(jnp.bfloat16)
        carry = carry + jnp.dot(act.T, slotted_part, preferred_element_type=jnp.float32)
        return carry, hidden

    weight_sum, hidden = lax.scan(
        merger_group,
        jnp.zeros((HID, OUTW), jnp.float32),
        (slotted.reshape(N_DP * N_CTX, SLOTS, OUTW), merger_pre.reshape(N_DP * N_CTX, SLOTS, HID)),
    )
    hidden_grad = hidden.reshape(N_DP * N_CTX * SLOTS, HID)
    weight_grad = weight_sum * (TOKENS ** -0.5)

    blocks = PATCHES // PATCH_DEV
    stacked = (
        query.reshape(blocks, PATCH_DEV, D),
        key_states.reshape(blocks, PATCH_DEV, D),
        value_states.reshape(blocks, PATCH_DEV, D),
        out_grad.reshape(blocks, PATCH_DEV, D),
        jnp.transpose(position.reshape(2, blocks, PATCH_DEV), (1, 0, 2)),
    )

    def one_block(items):
        return attention_block(items[0], items[1], items[2], items[3], items[4])

    query_grad, key_grad, value_grad = lax.map(one_block, stacked)
    return (
        hidden_grad,
        weight_grad,
        query_grad.reshape(PATCHES, D),
        key_grad.reshape(PATCHES, D),
        value_grad.reshape(PATCHES, D),
    )
```

```python
import functools
import math

import jax
import jax.numpy as jnp
from jax import lax
from jax.experimental import pallas as pl
from jax.experimental.pallas import tpu as pltpu
from jax.sharding import Mesh
from jax.sharding import PartitionSpec as P

HEAD = 80
WIN = 64
CTX = ("y", "z")
DP = ("x", "k")
ALL = ("x", "k", "y", "z")
F32 = jnp.float32
BF16 = jnp.bfloat16
MIB = 1024 * 1024


def iota(shape, dim):
    return lax.broadcasted_iota(jnp.int32, shape, dim)


def mm(a, b):
    return lax.dot_general(a, b, (((1,), (0,)), ((), ())), preferred_element_type=F32)


def mm_nt(a, b):
    return lax.dot_general(a, b, (((1,), (1,)), ((), ())), preferred_element_type=F32)


def mm_tn(a, b):
    return lax.dot_general(a, b, (((0,), (0,)), ((), ())), preferred_element_type=F32)


def shifted(n, s):
    return [(i, (i + s) % n) for i in range(n)]


def after(v, *others):
    return lax.optimization_barrier((v, *others))[0]


def params(mib=40):
    return pltpu.CompilerParams(vmem_limit_bytes=mib * MIB)


def cost(flops, nbytes, trans=0):
    return pl.CostEstimate(flops=flops, bytes_accessed=nbytes, transcendentals=trans)


def pack_kernel(cap, own_ref, grad_ref, out_ref):
    rows, width = grad_ref.shape
    places = out_ref.shape[0]
    owner = own_ref[...]
    onehot = (owner == iota((rows, 128), 1)).astype(F32)
    earlier = (iota((rows, rows), 0) > iota((rows, rows), 1)).astype(BF16)
    before = mm(earlier, onehot.astype(BF16))
    rank = jnp.sum(before * onehot, axis=1, keepdims=True).astype(jnp.int32)
    target = owner * cap + rank
    select = (target == iota((rows, places), 1)).astype(F32).T.astype(BF16)
    out_ref[:, :width] = mm(select, grad_ref[...]).astype(BF16)
    out_ref[:, width:] = mm(select, jnp.ones((rows, 128), BF16)).astype(BF16)


def packed(owner, grad, places, cap):
    rows, width = grad.shape
    return pl.pallas_call(
        functools.partial(pack_kernel, cap),
        out_shape=jax.ShapeDtypeStruct((places, width + 128), BF16),
        compiler_params=params(),
        cost_estimate=cost(2 * places * rows * width, 2 * (places + rows) * width),
        name="pack",
    )(owner, grad)


def land_kernel(inc_ref, out_ref, blocks_ref):
    slots, width = out_ref.shape
    parts, part, _ = blocks_ref.shape
    flags = inc_ref[:, width:].astype(F32).T.astype(BF16)
    earlier = (iota((slots, slots), 0) < iota((slots, slots), 1)).astype(BF16)
    slot = mm(flags[:16], earlier)[:1].astype(jnp.int32)
    here = flags[:1].astype(F32) > 0.5
    slot = jnp.where(here, slot, -1)
    landing = (iota((slots, slots), 0) == slot).astype(BF16)
    rows = mm(landing, inc_ref[:, :width])
    out_ref[...] = rows.astype(BF16)
    blocks_ref[...] = rows.T.astype(BF16).reshape(blocks_ref.shape)


def landed(incoming, parts):
    slots, wide = incoming.shape
    width = wide - 128
    return pl.pallas_call(
        land_kernel,
        out_shape=(
            jax.ShapeDtypeStruct((slots, width), BF16),
            jax.ShapeDtypeStruct((parts, width // parts, slots), BF16),
        ),
        compiler_params=params(),
        cost_estimate=cost(2 * slots * slots * width, 6 * slots * width),
        name="land",
    )(incoming)


def act_kernel(pre_ref, out_ref):
    x = pre_ref[...].astype(F32)
    act = x * (0.5 * (1.0 + lax.erf(x * 0.5**0.5)))
    out_ref[...] = act.T.astype(BF16)


def activated(pre):
    slots, hid = pre.shape
    block = hid // 4
    return pl.pallas_call(
        act_kernel,
        grid=(4,),
        in_specs=[pl.BlockSpec((slots, block), lambda i: (0, i))],
        out_specs=pl.BlockSpec((block, slots), lambda i: (i, 0)),
        out_shape=jax.ShapeDtypeStruct((hid, slots), BF16),
        compiler_params=params(),
        cost_estimate=cost(40 * slots * hid, 4 * slots * hid),
        name="act",
    )(pre)


def hidden_kernel(at_ref, slot_ref, pre_ref, *refs):
    *lines, out_ref, held, sems = refs
    step = pl.program_id(0)
    owners = at_ref.shape[0] // 4

    @pl.when(step == 0)
    def _():
        first = 0
        copies = []
        for i, ref in enumerate(lines):
            count = ref.shape[0]
            into = held.at[pl.ds(first, count)]
            copies.append(pltpu.make_async_copy(ref, into, sems.at[i]))
            first += count
        for copy in copies:
            copy.start()
        for copy in copies:
            copy.wait()

    rows = [held[at_ref[step * owners + i]] for i in range(owners)]
    linear = mm_nt(slot_ref[...], jnp.concatenate(rows, axis=0))
    x = pre_ref[...].astype(F32)
    slope = 0.5 * (1.0 + lax.erf(x * 0.5**0.5))
    slope = slope + x * jnp.exp(-0.5 * x * x) * (2.0 * math.pi) ** -0.5
    out_ref[...] = (linear * slope).astype(BF16)


def hidden_of(at, slotted, pre, lines):
    slots, width = slotted.shape
    hid = pre.shape[1]
    block = hid // 4
    return pl.pallas_call(
        hidden_kernel,
        grid_spec=pltpu.PrefetchScalarGridSpec(
            num_scalar_prefetch=1,
            grid=(4,),
            in_specs=[
                pl.BlockSpec((slots, width), lambda i, s: (0, 0)),
                pl.BlockSpec((slots, block), lambda i, s: (0, i)),
                *[pl.BlockSpec(memory_space=pl.ANY)] * len(lines),
            ],
            out_specs=pl.BlockSpec((slots, block), lambda i, s: (0, i)),
            scratch_shapes=[
                pltpu.VMEM((at.shape[0], *lines[0].shape[1:]), BF16),
                pltpu.SemaphoreType.DMA((len(lines),)),
            ],
        ),
        out_shape=jax.ShapeDtypeStruct((slots, hid), BF16),
        compiler_params=params(58),
        cost_estimate=cost(2 * slots * width * hid, 2 * (hid * width + 2 * slots * hid)),
        name="hidden",
    )(at, slotted, pre, *lines)


def weight_kernel(scale, idx_ref, cols_ref, own, mine, other, mine_half, other_half, *refs):
    outs, cols = refs[:5], refs[5]
    step = pl.program_id(0)
    slots = own.shape[2]

    @pl.when(step == 0)
    def _():
        for j in range(8):
            cols[j * slots : (j + 1) * slots] = cols_ref[idx_ref[j]].astype(F32).T.astype(BF16)

    ours = idx_ref[12 + step] == 1
    across = [jnp.where(ours, mine_half[i], other_half[1 - i]) for i in (0, 1)]
    rows = [own[0], own[1], mine[0], mine[1], other[0], other[1], *across]
    total = mm(jnp.concatenate(rows, axis=1), cols[...]) * scale

    @pl.when(step == 0)
    def _():
        cut = total.shape[0] // 2
        outs[0][...] = total[:cut]
        outs[1][...] = total[cut:]

    for q in range(3):

        @pl.when(step == q + 1)
        def _(q=q):
            cut = total.shape[0] // 2
            outs[2 + q][0] = total[:cut]
            outs[2 + q][1] = total[cut:]


def weight_rows(idx, cols, own, mine, other, mine_half, other_half, scale):
    _, hid, slots = own.shape
    part = cols.shape[1]
    block = hid // 4

    def whole(shape):
        return pl.BlockSpec(shape, lambda i, s: (0,) * len(shape))

    full = pl.BlockSpec((2, block, slots), lambda i, s: (0, s[8 + i], 0))
    half = pl.BlockSpec((2, block, slots), lambda i, s: (0, s[8 + i] % 2, 0))
    shapes = [(block // 2, part)] * 2 + [(2, block // 2, part)] * 3
    return pl.pallas_call(
        functools.partial(weight_kernel, scale),
        grid_spec=pltpu.PrefetchScalarGridSpec(
            num_scalar_prefetch=1,
            grid=(4,),
            in_specs=[whole(cols.shape), full, full, full, half, half],
            out_specs=[whole(shape) for shape in shapes],
            scratch_shapes=[pltpu.VMEM((8 * slots, part), BF16)],
        ),
        out_shape=[jax.ShapeDtypeStruct(shape, F32) for shape in shapes],
        compiler_params=params(),
        cost_estimate=cost(2 * hid * slots * 8 * part, 2 * hid * slots * 8 + 4 * hid * part),
        name="weight",
    )(idx, cols, own, mine, other, mine_half, other_half)


def add_kernel(rows_ref, add_ref, out_ref):
    out_ref[0] = rows_ref[0] + add_ref[...]


def added(rows, addend, at):
    block = pl.BlockSpec((1, *addend.shape), lambda i: (at, 0, 0))
    return pl.pallas_call(
        add_kernel,
        grid=(1,),
        in_specs=[block, pl.BlockSpec(addend.shape, lambda i: (0, 0))],
        out_specs=block,
        out_shape=jax.ShapeDtypeStruct(rows.shape, rows.dtype),
        input_output_aliases={0: 0},
        compiler_params=params(),
        cost_estimate=cost(addend.size, 12 * addend.size),
        name="add",
    )(rows, addend)


def attention_kernel(q_ref, k_ref, v_ref, g_ref, cos_ref, sin_ref, *refs):
    qg_ref, kg_ref, vg_ref, *scratch = refs[-7:]
    qr_ref, kr_ref = scratch[:2]
    dq_ref, dk_ref = scratch[2:]
    win, width = q_ref.shape
    half_width = width // 2
    factor = HEAD**-0.5
    lane = iota((win, half_width), 1)
    first = lane % HEAD < HEAD // 2
    count = HEAD // 2
    spread = (iota((count, half_width), 1) % count == iota((count, half_width), 0)).astype(F32)

    def spread_out(table):
        dims = (((1,), (0,)), ((), ()))
        return lax.dot_general(
            table, spread, dims, precision=lax.Precision.HIGHEST, preferred_element_type=F32
        )

    cos = spread_out(cos_ref[...])
    sin = spread_out(sin_ref[...])
    sin = jnp.where(first, -sin, sin)

    def turned(x):
        left = pltpu.roll(x, half_width - HEAD // 2, 1)
        right = pltpu.roll(x, HEAD // 2, 1)
        return jnp.where(first, left, right) * sin

    for s in range(2):
        at = pl.ds(s * half_width, half_width)
        for src, dst in ((q_ref, qr_ref), (k_ref, kr_ref)):
            x = src[:, at].astype(F32)
            dst[:, at] = (x * cos + turned(x)).astype(BF16)
    wide = 256
    span = iota((win, wide), 1)
    for pair in range(width // (2 * HEAD)):
        start = pair * 2 * HEAD
        base = start // 128 * 128
        at = pl.ds(base, wide)
        lo = start - base
        one = (span >= lo) & (span < lo + HEAD)
        two = (span >= lo + HEAD) & (span < lo + 2 * HEAD)

        def stacked(x):
            x = x.astype(F32)
            zero = jnp.zeros_like(x)
            return jnp.concatenate([jnp.where(one, x, zero), jnp.where(two, x, zero)], 0).astype(BF16)

        q2 = stacked(qr_ref[:, at])
        g2 = stacked(g_ref[:, at])
        kk = kr_ref[:, at]
        scores = mm_nt(kk, q2)
        top = jnp.max(scores, axis=0, keepdims=True)
        e = jnp.exp((scores - top) * factor)
        probs = e * (1.0 / jnp.sum(e, axis=0, keepdims=True))
        probs_b = probs.astype(BF16)
        prob_grad = mm_nt(v_ref[:, at], g2)
        delta = jnp.sum(probs_b.astype(F32) * prob_grad, axis=0, keepdims=True)
        score_f = probs * (prob_grad - delta)
        score_grad = score_f.astype(BF16)
        vg = mm(probs_b, g2)
        kg = mm(score_grad, q2)
        qg = mm(score_f.T.astype(BF16), kk)
        qg = jnp.where(one, qg[:win], qg[win:])
        both = one | two
        for ref, val in ((vg_ref, vg), (dk_ref, kg), (dq_ref, qg)):
            if lo:
                old = ref[:, pl.ds(base, 128)]
                new = jnp.where(both[:, :128], val[:, :128].astype(old.dtype), old)
                ref[:, pl.ds(base, 128)] = new
                ref[:, pl.ds(base + 128, 128)] = val[:, 128:].astype(old.dtype)
            else:
                ref[:, at] = val.astype(ref.dtype)
    for s in range(2):
        at = pl.ds(s * half_width, half_width)
        for src, dst in ((dq_ref, qg_ref), (dk_ref, kg_ref)):
            x = src[:, at] * factor
            dst[:, at] = (x * cos - turned(x)).astype(BF16)


def attention(first, windows, query, key_states, value_states, out_grad, cos, sin, *earlier):
    count, width = query.shape
    block = pl.BlockSpec((WIN, width), lambda w: (w + first, 0))
    table = pl.BlockSpec((WIN, HEAD // 2), lambda w: (w + first, 0))
    out = jax.ShapeDtypeStruct((count, width), BF16)
    return pl.pallas_call(
        attention_kernel,
        grid=(windows,),
        in_specs=[block] * 4 + [table] * 2 + [pl.BlockSpec(memory_space=pl.ANY)] * len(earlier),
        out_specs=[block] * 3,
        out_shape=[out] * 3,
        scratch_shapes=[pltpu.VMEM((WIN, width), BF16)] * 2 + [pltpu.VMEM((WIN, width), F32)] * 2,
        input_output_aliases={6 + i: i for i in range(len(earlier))},
        compiler_params=params(58),
        cost_estimate=cost(160 * windows * WIN * WIN * width, 18 * windows * WIN * width),
        name="attention",
    )(query, key_states, value_states, out_grad, cos, sin, *earlier)


def rope_tables(position):
    quarter = HEAD // 4
    freq = 1.0 / 10000.0 ** (jnp.arange(quarter, dtype=F32) * (4.0 / HEAD))
    rows = position[0].astype(F32)[:, None] * freq[None, :]
    cols = position[1].astype(F32)[:, None] * freq[None, :]
    angles = jnp.concatenate([rows, cols], axis=1)
    return jnp.cos(angles), jnp.sin(angles)


def shards(merged_grad, merged_owner, pre, fc2, query, key_states, value_states, out_grad, position):
    owners, replicas = lax.axis_size(CTX), lax.axis_size(DP)
    xs, ys, zs = (lax.axis_size(axis) for axis in ("x", "y", "z"))
    x, k, y, z = (lax.axis_index(axis) for axis in ALL)
    slots, hid = pre.shape
    rows_here = merged_grad.shape[0]
    cap = slots // owners

    def hop(v, axis, by):
        return lax.ppermute(v, axis, shifted(lax.axis_size(axis), by))

    def apart(v, axis):
        n = lax.axis_size(axis)
        steps = [(core, i, (i + 1 - 2 * core) % n) for core in (0, 1) for i in range(n)]
        if axis == "x":
            return lax.ppermute(v, DP, [(2 * i + core, 2 * j + core) for core, i, j in steps])
        return lax.ppermute(v, ("k", axis), [(n * core + i, n * core + j) for core, i, j in steps])

    def numbers(*values):
        return jnp.stack(values).astype(jnp.int32)

    outgoing = packed(merged_owner, merged_grad, slots, cap)
    incoming = lax.all_to_all(
        outgoing.reshape(owners, cap, -1), CTX, split_axis=0, concat_axis=0, tiled=True
    )

    act = activated(after(pre, outgoing))
    own = jnp.stack([act, hop(act, "k", 1)])
    mine = apart(own, "x")

    line = after(fc2, act)
    beside = [hop(line, "y", by) for by in range(1, ys)]

    tables = rope_tables(position)
    grads = attention(0, 2, after(query, act), key_states, value_states, out_grad, *tables)

    grads = attention(
        2, 2, after(query, own), key_states, value_states, out_grad, *tables, *grads
    )
    mine = after(mine, *grads, *beside)
    mine_half = lax.dynamic_slice_in_dim(mine, k * (hid // 2), hid // 2, axis=1)
    mine_half = apart(mine_half, "x")

    slotted, blocks = landed(after(incoming, *grads).reshape(slots, -1), replicas)
    cols = lax.all_to_all(blocks, DP, split_axis=0, concat_axis=0, tiled=True)
    mine_half = after(mine_half, cols)
    other, other_half = hop(mine, "k", 1), hop(mine_half, "k", 1)

    before, behind = (x - 1 + 2 * k) % xs, (x + 1 - 2 * k) % xs
    places = []
    for there, core in ((x, k), (before, k), (behind, 1 - k), ((x + 2) % xs, k)):
        places += [2 * there + core, 2 * there + 1 - core]
    quarters = [(y + dy) % ys for dy in (2, 1, 3, 0)]
    ours = [(q < 2) == (k == 0) for q in quarters]
    factor = (rows_here * owners * replicas) ** (-0.5)
    idx = numbers(*places, *quarters, *ours)
    top, bottom, above, below, here = weight_rows(
        idx, cols, own, mine, other, mine_half, other_half, factor
    )
    from_below, from_above = hop(top, "y", 1), hop(bottom, "y", -1)
    above = hop(added(above, from_below, 0), "y", 1)
    below = hop(added(below, from_above, 1), "y", -1)

    line = jnp.stack([line, *beside])
    ones = [apart(after(line, slotted), "z")]
    ones.append(apart(ones[0], "z"))
    ones.append(apart(after(ones[1], from_below, from_above), "z"))
    last = lax.dynamic_slice_in_dim(ones[2], k * (ys // 2), ys // 2, axis=0)
    ones.append(apart(last, "z"))
    lines = [line, *ones, *(hop(part, "k", 1) for part in ones)]

    turn = (y - jnp.arange(ys))[:, None] % ys
    away = (jnp.arange(zs)[None, :] - z) % zs
    by_core = jnp.where(away == 4, turn >= 2, away < 4).astype(jnp.int32)
    step = jnp.where(away < 4, away, zs - away)
    at = jnp.where(away == 4, 12 + turn % 2, 4 * step - 4 + turn)
    at = jnp.where(by_core == k, 4, 18) + at
    at = jnp.where(away == 0, turn, at).astype(jnp.int32).reshape(-1)
    hidden_grad = hidden_of(at, slotted, pre, lines)

    total = here + above + below
    pieces = total.reshape(zs, hid // owners, -1)
    pieces = lax.all_to_all(pieces, "z", split_axis=0, concat_axis=0, tiled=True)
    weight_grad = jnp.sum(after(pieces, hidden_grad), axis=0)
    return (hidden_grad, weight_grad, *grads)


def solution(mesh):
    finer = Mesh(mesh.devices.reshape(4, 2, 4, 8), ALL)
    rows = P(ALL, None)
    return jax.shard_map(
        shards,
        mesh=finer,
        in_specs=(rows, rows, rows, P(CTX, None), rows, rows, rows, rows, P(None, ALL)),
        out_specs=(rows, P(CTX, DP), rows, rows, rows),
        check_vma=False,
    )
```

```python
import functools
import math

import jax
import jax.numpy as jnp
from jax import lax
from jax.experimental import pallas as pl
from jax.experimental.pallas import tpu as pltpu
from jax.sharding import Mesh
from jax.sharding import PartitionSpec as P

HEAD = 80
WIN = 64
CTX = ("y", "z")
DP = ("x", "k")
ALL = ("x", "k", "y", "z")
F32 = jnp.float32
BF16 = jnp.bfloat16
MIB = 1024 * 1024


def iota(shape, dim):
    return lax.broadcasted_iota(jnp.int32, shape, dim)


def mm(a, b):
    return lax.dot_general(a, b, (((1,), (0,)), ((), ())), preferred_element_type=F32)


def mm_nt(a, b):
    return lax.dot_general(a, b, (((1,), (1,)), ((), ())), preferred_element_type=F32)


def mm_tn(a, b):
    return lax.dot_general(a, b, (((0,), (0,)), ((), ())), preferred_element_type=F32)


def shifted(n, s):
    return [(i, (i + s) % n) for i in range(n)]


def after(v, *others):
    return lax.optimization_barrier((v, *others))[0]


def params(mib=40):
    return pltpu.CompilerParams(vmem_limit_bytes=mib * MIB)


def cost(flops, nbytes, trans=0):
    return pl.CostEstimate(flops=flops, bytes_accessed=nbytes, transcendentals=trans)


def pack_kernel(cap, own_ref, grad_ref, out_ref):
    rows, width = grad_ref.shape
    places = out_ref.shape[0]
    owner = own_ref[...]
    onehot = (owner == iota((rows, 128), 1)).astype(F32)
    earlier = (iota((rows, rows), 0) > iota((rows, rows), 1)).astype(BF16)
    before = mm(earlier, onehot.astype(BF16))
    rank = jnp.sum(before * onehot, axis=1, keepdims=True).astype(jnp.int32)
    target = owner * cap + rank
    select = (target == iota((rows, places), 1)).astype(F32).T.astype(BF16)
    out_ref[:, :width] = mm(select, grad_ref[...]).astype(BF16)
    out_ref[:, width:] = mm(select, jnp.ones((rows, 128), BF16)).astype(BF16)


def packed(owner, grad, places, cap):
    rows, width = grad.shape
    return pl.pallas_call(
        functools.partial(pack_kernel, cap),
        out_shape=jax.ShapeDtypeStruct((places, width + 128), BF16),
        compiler_params=params(),
        cost_estimate=cost(2 * places * rows * width, 2 * (places + rows) * width),
        name="pack",
    )(owner, grad)


def land_kernel(inc_ref, out_ref, blocks_ref):
    slots, width = out_ref.shape
    parts, part, _ = blocks_ref.shape
    flags = inc_ref[:, width:].astype(F32).T.astype(BF16)
    earlier = (iota((slots, slots), 0) < iota((slots, slots), 1)).astype(BF16)
    slot = mm(flags[:16], earlier)[:1].astype(jnp.int32)
    here = flags[:1].astype(F32) > 0.5
    slot = jnp.where(here, slot, -1)
    landing = (iota((slots, slots), 0) == slot).astype(BF16)
    rows = mm(landing, inc_ref[:, :width])
    out_ref[...] = rows.astype(BF16)
    blocks_ref[...] = rows.T.astype(BF16).reshape(blocks_ref.shape)


def landed(incoming, parts):
    slots, wide = incoming.shape
    width = wide - 128
    return pl.pallas_call(
        land_kernel,
        out_shape=(
            jax.ShapeDtypeStruct((slots, width), BF16),
            jax.ShapeDtypeStruct((parts, width // parts, slots), BF16),
        ),
        compiler_params=params(58),
        cost_estimate=cost(2 * slots * slots * width, 6 * slots * width),
        name="land",
    )(incoming)


def act_kernel(pre_ref, out_ref):
    x = pre_ref[...].astype(F32)
    act = x * (0.5 * (1.0 + lax.erf(x * 0.5**0.5)))
    out_ref[...] = act.T.astype(BF16)


def activated(pre):
    slots, hid = pre.shape
    block = hid // 4
    return pl.pallas_call(
        act_kernel,
        grid=(4,),
        in_specs=[pl.BlockSpec((slots, block), lambda i: (0, i))],
        out_specs=pl.BlockSpec((block, slots), lambda i: (i, 0)),
        out_shape=jax.ShapeDtypeStruct((hid, slots), BF16),
        compiler_params=params(),
        cost_estimate=cost(40 * slots * hid, 4 * slots * hid),
        name="act",
    )(pre)


def hidden_kernel(at_ref, slot_ref, pre_ref, *refs):
    *lines, out_ref, held, sems = refs
    step = pl.program_id(0)
    owners = at_ref.shape[0] // 4

    @pl.when(step == 0)
    def _():
        first = 0
        copies = []
        for i, ref in enumerate(lines):
            count = ref.shape[0]
            into = held.at[pl.ds(first, count)]
            copies.append(pltpu.make_async_copy(ref, into, sems.at[i]))
            first += count
        for copy in copies:
            copy.start()
        for copy in copies:
            copy.wait()

    rows = [held[at_ref[step * owners + i]] for i in range(owners)]
    linear = mm_nt(slot_ref[...], jnp.concatenate(rows, axis=0))
    x = pre_ref[...].astype(F32)
    slope = 0.5 * (1.0 + lax.erf(x * 0.5**0.5))
    slope = slope + x * jnp.exp(-0.5 * x * x) * (2.0 * math.pi) ** -0.5
    out_ref[...] = (linear * slope).astype(BF16)


def hidden_of(at, slotted, pre, lines):
    slots, width = slotted.shape
    hid = pre.shape[1]
    block = hid // 4
    return pl.pallas_call(
        hidden_kernel,
        grid_spec=pltpu.PrefetchScalarGridSpec(
            num_scalar_prefetch=1,
            grid=(4,),
            in_specs=[
                pl.BlockSpec((slots, width), lambda i, s: (0, 0)),
                pl.BlockSpec((slots, block), lambda i, s: (0, i)),
                *[pl.BlockSpec(memory_space=pl.ANY)] * len(lines),
            ],
            out_specs=pl.BlockSpec((slots, block), lambda i, s: (0, i)),
            scratch_shapes=[
                pltpu.VMEM((at.shape[0], *lines[0].shape[1:]), BF16),
                pltpu.SemaphoreType.DMA((len(lines),)),
            ],
        ),
        out_shape=jax.ShapeDtypeStruct((slots, hid), BF16),
        compiler_params=params(58),
        cost_estimate=cost(2 * slots * width * hid, 2 * (hid * width + 2 * slots * hid)),
        name="hidden",
    )(at, slotted, pre, *lines)


def weight_kernel(scale, idx_ref, cols_ref, own, mine, other, mine_half, other_half, *refs):
    *outs, cols = refs
    count = pl.num_programs(0)
    step = pl.program_id(0)
    slots = own.shape[2]

    @pl.when(step == 0)
    def _():
        for j in range(8):
            cols[j * slots : (j + 1) * slots] = cols_ref[idx_ref[j]].astype(F32).T.astype(BF16)

    ours = idx_ref[8 + count + step] == 1
    across = [jnp.where(ours, mine_half[i], other_half[1 - i]) for i in (0, 1)]
    rows = [own[0], own[1], mine[0], mine[1], other[0], other[1], *across]
    total = mm(jnp.concatenate(rows, axis=1), cols[...]) * scale

    cut = total.shape[0] // 2
    for q, out in enumerate(outs):

        @pl.when(step == q)
        def _(out=out):
            out[0] = total[:cut]
            out[1] = total[cut:]


def weight_rows(idx, cols, own, mine, other, mine_half, other_half, scale):
    _, hid, slots = own.shape
    part = cols.shape[1]
    block = hid // 4
    count = (idx.shape[0] - 8) // 2

    def whole(shape):
        return pl.BlockSpec(shape, lambda i, s: (0,) * len(shape))

    full = pl.BlockSpec((2, block, slots), lambda i, s: (0, s[8 + i], 0))
    half = pl.BlockSpec((2, block, slots), lambda i, s: (0, s[8 + i] % 2, 0))
    shapes = [(2, block // 2, part)] * count
    return pl.pallas_call(
        functools.partial(weight_kernel, scale),
        grid_spec=pltpu.PrefetchScalarGridSpec(
            num_scalar_prefetch=1,
            grid=(count,),
            in_specs=[whole(cols.shape), full, full, full, half, half],
            out_specs=[whole(shape) for shape in shapes],
            scratch_shapes=[pltpu.VMEM((8 * slots, part), BF16)],
        ),
        out_shape=[jax.ShapeDtypeStruct(shape, F32) for shape in shapes],
        compiler_params=params(),
        cost_estimate=cost(2 * count * block * slots * 8 * part, 16 * count * block * slots),
        name="weight",
    )(idx, cols, own, mine, other, mine_half, other_half)


def add_kernel(above_ref, below_ref, low_ref, high_ref, above_out, below_out):
    above_out[0] = above_ref[0] + low_ref[...]
    below_out[0] = below_ref[0] + high_ref[...]


def added(above, below, low, high):
    whole = pl.BlockSpec(low.shape, lambda i: (0, 0))
    first = pl.BlockSpec((1, *low.shape), lambda i: (0, 0, 0))
    second = pl.BlockSpec((1, *low.shape), lambda i: (1, 0, 0))
    return pl.pallas_call(
        add_kernel,
        grid=(1,),
        in_specs=[first, second, whole, whole],
        out_specs=[first, second],
        out_shape=[jax.ShapeDtypeStruct(above.shape, above.dtype)] * 2,
        input_output_aliases={0: 0, 1: 1},
        compiler_params=params(),
        cost_estimate=cost(2 * low.size, 24 * low.size),
        name="add",
    )(above, below, low, high)


def attention_kernel(q_ref, k_ref, v_ref, g_ref, cos_ref, sin_ref, *refs):
    qg_ref, kg_ref, vg_ref, *scratch = refs[-7:]
    qr_ref, kr_ref = scratch[:2]
    dq_ref, dk_ref = scratch[2:]
    win, width = q_ref.shape
    half_width = width // 2
    factor = HEAD**-0.5
    lane = iota((win, half_width), 1)
    first = lane % HEAD < HEAD // 2
    count = HEAD // 2
    spread = (iota((count, half_width), 1) % count == iota((count, half_width), 0)).astype(F32)

    def spread_out(table):
        dims = (((1,), (0,)), ((), ()))
        return lax.dot_general(
            table, spread, dims, precision=lax.Precision.HIGHEST, preferred_element_type=F32
        )

    cos = spread_out(cos_ref[...])
    sin = spread_out(sin_ref[...])
    sin = jnp.where(first, -sin, sin)

    def turned(x):
        left = pltpu.roll(x, half_width - HEAD // 2, 1)
        right = pltpu.roll(x, HEAD // 2, 1)
        return jnp.where(first, left, right) * sin

    for s in range(2):
        at = pl.ds(s * half_width, half_width)
        for src, dst in ((q_ref, qr_ref), (k_ref, kr_ref)):
            x = src[:, at].astype(F32)
            dst[:, at] = (x * cos + turned(x)).astype(BF16)
    wide = 256
    span = iota((win, wide), 1)
    for pair in range(width // (2 * HEAD)):
        start = pair * 2 * HEAD
        base = start // 128 * 128
        at = pl.ds(base, wide)
        lo = start - base
        one = (span >= lo) & (span < lo + HEAD)
        two = (span >= lo + HEAD) & (span < lo + 2 * HEAD)

        def stacked(x):
            x = x.astype(F32)
            zero = jnp.zeros_like(x)
            return jnp.concatenate([jnp.where(one, x, zero), jnp.where(two, x, zero)], 0).astype(BF16)

        q2 = stacked(qr_ref[:, at])
        g2 = stacked(g_ref[:, at])
        kk = kr_ref[:, at]
        scores = mm_nt(kk, q2)
        top = jnp.max(scores, axis=0, keepdims=True)
        e = jnp.exp((scores - top) * factor)
        probs = e * (1.0 / jnp.sum(e, axis=0, keepdims=True))
        probs_b = probs.astype(BF16)
        prob_grad = mm_nt(v_ref[:, at], g2)
        delta = jnp.sum(probs_b.astype(F32) * prob_grad, axis=0, keepdims=True)
        score_f = probs * (prob_grad - delta)
        score_grad = score_f.astype(BF16)
        vg = mm(probs_b, g2)
        kg = mm(score_grad, q2)
        qg = mm(score_f.T.astype(BF16), kk)
        qg = jnp.where(one, qg[:win], qg[win:])
        both = one | two
        for ref, val in ((vg_ref, vg), (dk_ref, kg), (dq_ref, qg)):
            if lo:
                old = ref[:, pl.ds(base, 128)]
                new = jnp.where(both[:, :128], val[:, :128].astype(old.dtype), old)
                ref[:, pl.ds(base, 128)] = new
                ref[:, pl.ds(base + 128, 128)] = val[:, 128:].astype(old.dtype)
            else:
                ref[:, at] = val.astype(ref.dtype)
    for s in range(2):
        at = pl.ds(s * half_width, half_width)
        for src, dst in ((dq_ref, qg_ref), (dk_ref, kg_ref)):
            x = src[:, at] * factor
            dst[:, at] = (x * cos - turned(x)).astype(BF16)


def attention(first, windows, query, key_states, value_states, out_grad, cos, sin, *earlier):
    count, width = query.shape
    block = pl.BlockSpec((WIN, width), lambda w: (w + first, 0))
    table = pl.BlockSpec((WIN, HEAD // 2), lambda w: (w + first, 0))
    out = jax.ShapeDtypeStruct((count, width), BF16)
    return pl.pallas_call(
        attention_kernel,
        grid=(windows,),
        in_specs=[block] * 4 + [table] * 2 + [pl.BlockSpec(memory_space=pl.ANY)] * len(earlier),
        out_specs=[block] * 3,
        out_shape=[out] * 3,
        scratch_shapes=[pltpu.VMEM((WIN, width), BF16)] * 2 + [pltpu.VMEM((WIN, width), F32)] * 2,
        input_output_aliases={6 + i: i for i in range(len(earlier))},
        compiler_params=params(58),
        cost_estimate=cost(160 * windows * WIN * WIN * width, 18 * windows * WIN * width),
        name="attention",
    )(query, key_states, value_states, out_grad, cos, sin, *earlier)


def rope_tables(position):
    quarter = HEAD // 4
    freq = 1.0 / 10000.0 ** (jnp.arange(quarter, dtype=F32) * (4.0 / HEAD))
    rows = position[0].astype(F32)[:, None] * freq[None, :]
    cols = position[1].astype(F32)[:, None] * freq[None, :]
    angles = jnp.concatenate([rows, cols], axis=1)
    return jnp.cos(angles), jnp.sin(angles)


def shards(merged_grad, merged_owner, pre, fc2, query, key_states, value_states, out_grad, position):
    owners, replicas = lax.axis_size(CTX), lax.axis_size(DP)
    xs, ys, zs = (lax.axis_size(axis) for axis in ("x", "y", "z"))
    x, k, y, z = (lax.axis_index(axis) for axis in ALL)
    slots, hid = pre.shape
    rows_here = merged_grad.shape[0]
    cap = slots // owners

    def hop(v, axis, by):
        return lax.ppermute(v, axis, shifted(lax.axis_size(axis), by))

    def apart(v, axis):
        n = lax.axis_size(axis)
        steps = [(core, i, (i + 1 - 2 * core) % n) for core in (0, 1) for i in range(n)]
        if axis == "x":
            return lax.ppermute(v, DP, [(2 * i + core, 2 * j + core) for core, i, j in steps])
        return lax.ppermute(v, ("k", axis), [(n * core + i, n * core + j) for core, i, j in steps])

    def numbers(*values):
        return jnp.stack(values).astype(jnp.int32)

    outgoing = packed(merged_owner, merged_grad, slots, cap)
    incoming = lax.all_to_all(
        outgoing.reshape(owners, cap, -1), CTX, split_axis=0, concat_axis=0, tiled=True
    )

    act = activated(after(pre, outgoing))
    own = jnp.stack([act, hop(act, "k", 1)])
    mine = apart(own, "x")

    line = after(fc2, act)
    beside = [hop(line, "y", by) for by in range(1, ys)]

    tables = rope_tables(position)
    grads = attention(0, 2, after(query, act), key_states, value_states, out_grad, *tables)

    grads = attention(
        2, 2, after(query, own), key_states, value_states, out_grad, *tables, *grads
    )
    mine = after(mine, *grads, *beside)
    mine_half = lax.dynamic_slice_in_dim(mine, k * (hid // 2), hid // 2, axis=1)
    mine_half = apart(mine_half, "x")

    slotted, blocks = landed(after(incoming, *grads).reshape(slots, -1), replicas)
    cols = lax.all_to_all(blocks, DP, split_axis=0, concat_axis=0, tiled=True)
    mine_half = after(mine_half, cols)
    other, other_half = hop(mine, "k", 1), hop(mine_half, "k", 1)

    before, behind = (x - 1 + 2 * k) % xs, (x + 1 - 2 * k) % xs
    places = []
    for there, core in ((x, k), (before, k), (behind, 1 - k), ((x + 2) % xs, k)):
        places += [2 * there + core, 2 * there + 1 - core]
    factor = (rows_here * owners * replicas) ** (-0.5)

    def rows_of(steps, *earlier):
        quarters = [(y + dy) % ys for dy in steps]
        ours = [(q < 2) == (k == 0) for q in quarters]
        idx = after(numbers(*places, *quarters, *ours), *earlier)
        return weight_rows(idx, cols, own, mine, other, mine_half, other_half, factor)

    (across,) = rows_of((2,))
    from_below, from_above = hop(across[0], "y", 1), hop(across[1], "y", -1)
    above, below, here = rows_of((1, 3, 0), across)
    above, below = added(above, below, from_below, from_above)
    above, below = hop(above, "y", 1), hop(below, "y", -1)

    line = jnp.stack([line, *beside])
    ones = [apart(after(line, slotted), "z")]
    ones.append(apart(ones[0], "z"))
    ones.append(apart(after(ones[1], from_below, from_above, here), "z"))
    last = lax.dynamic_slice_in_dim(ones[2], k * (ys // 2), ys // 2, axis=0)
    ones.append(apart(last, "z"))
    lines = [line, *ones, *(hop(part, "k", 1) for part in ones)]

    turn = (y - jnp.arange(ys))[:, None] % ys
    away = (jnp.arange(zs)[None, :] - z) % zs
    by_core = jnp.where(away == 4, turn >= 2, away < 4).astype(jnp.int32)
    step = jnp.where(away < 4, away, zs - away)
    at = jnp.where(away == 4, 12 + turn % 2, 4 * step - 4 + turn)
    at = jnp.where(by_core == k, 4, 18) + at
    at = jnp.where(away == 0, turn, at).astype(jnp.int32).reshape(-1)
    hidden_grad = hidden_of(at, slotted, pre, lines)

    total = here + above + below
    pieces = total.reshape(zs, hid // owners, -1)
    pieces = lax.all_to_all(pieces, "z", split_axis=0, concat_axis=0, tiled=True)
    weight_grad = jnp.sum(after(pieces, hidden_grad), axis=0)
    return (hidden_grad, weight_grad, *grads)


def solution(mesh):
    finer = Mesh(mesh.devices.reshape(4, 2, 4, 8), ALL)
    rows = P(ALL, None)
    return jax.shard_map(
        shards,
        mesh=finer,
        in_specs=(rows, rows, rows, P(CTX, None), rows, rows, rows, rows, P(None, ALL)),
        out_specs=(rows, P(CTX, DP), rows, rows, rows),
        check_vma=False,
    )
```
